32 devices in a mesh: dp: 8 (over z, x), tensor: 4 (over y, core).
Axes of the slice: x: 2, y: 2, z: 4, core: 2. Of those that a mesh axis runs over, the one named last changes fastest.
Arguments:
- context: bfloat16 [8192, 7168], P('dp', 'tensor'), may hold values from -6 to 6
- resid: bfloat16 [8192, 7168], P(('dp', 'tensor')), may hold values from -6 to 6
- o_weight: bfloat16 [7168, 7168], P('tensor', 'dp'), may hold values from -0.0625 to 0.0625
- norm_gain: float32 [7168], replicated, may hold values from 0.5 to 1.5
- queries: float32 [32, 7168], P('dp'), may hold values from -6 to 6
- positive_ids: int32 [32], P('dp'), may hold values from 0 to 15
- negative_ids: int32 [32, 7], P('dp'), may hold values from 0 to 15
- margins: float32 [32, 7], P('dp'), may hold values from -6 to 6
- pair_counts: int32 [32], P('dp'), may hold values from 1 to 7, as said below
Outputs:
- hidden_grad: float32 [8192, 7168], P(('dp', 'tensor'))
- loss: float32 [], replicated
The draws below stay inside these ranges and needn't reach their ends.
Inputs may be any that keep to these rules, and one draw needn't show every extreme that they name: `pair_counts`: some query has all 7 negatives live.
All inputs are finite; a program needn't handle non-finite values.
Results may differ from the reference program's by a relative error of at most 0.0003.
Values may be sent and summed in bfloat16 or wider, within the bound.
A program may use at most 192 MiB of HBM per device.

```python
import jax
import jax.numpy as jnp
from jax import lax

D = 7168
SEQ = 512
PASS_DEV = 2
Q_DEV = 4
NEG = 7
NPASS = 16
QUERIES = 32
TOKENS = 8192
N_DP = 8
N_TENSOR = 4


def draw_pair_counts(key, part):
    counts = jax.random.randint(key, (QUERIES,), 1, NEG + 1)
    return counts.at[0].set(NEG).astype(jnp.int32)


def set_ends(drawn, stream_key, smallest, high):
    longest = drawn.shape.index(max(drawn.shape))
    spots = []
    for shift in (0, 1):
        where = [jax.random.randint(jax.random.fold_in(stream_key, axis), (), 0, length) for axis, length in enumerate(drawn.shape)]
        where[longest] = (where[longest] + shift) % drawn.shape[longest]
        spots.append(tuple(where))
    return drawn.at[spots[0]].set(smallest).at[spots[1]].set(high)


def steps_of(rng, shape, split, least, top_value):
    loudness, own = 1.0, jax.random.fold_in(rng, 6)
    for axis_at, parts in split:
        draws = jnp.exp(jax.random.uniform(jax.random.fold_in(own, axis_at), (parts,), jnp.float32, least / len(split), top_value / len(split)))
        loudness = loudness * jnp.repeat(draws, shape[axis_at] // parts).reshape([-1 if axis == axis_at else 1 for axis in range(len(shape))])
    return loudness


def bell_draw(stream_key, dims, scale, reach, split=(), kind=jnp.bfloat16):
    result = scale * jax.random.normal(stream_key, dims, jnp.float32)
    if split:
        result = result * steps_of(stream_key, dims, split, -0.22, 0.18)
    return jnp.clip(result, -reach, reach).astype(kind)


def setup_inputs(seed: int = 0) -> dict:
    arg_keys = jax.random.split(jax.random.key(seed), 10)
    return {
        "context": bell_draw(arg_keys[0], (TOKENS, D), 1.0, 6.0, ((0, 8), (1, 4))),
        "resid": bell_draw(arg_keys[1], (TOKENS, D), 1.0, 6.0, ((0, 32),)),
        "o_weight": bell_draw(arg_keys[2], (D, D), D ** -0.5, 0.0625, ((0, 4), (1, 8))),
        "norm_gain": jnp.clip(1.0 + 0.1 * jax.random.normal(arg_keys[3], (D,), jnp.float32), 0.5, 1.5),
        "queries": bell_draw(arg_keys[4], (QUERIES, D), 1.0, 6.0, ((0, 8),), jnp.float32),
        "positive_ids": set_ends(jax.random.randint(arg_keys[5], (QUERIES,), 0, NPASS), jax.random.fold_in(arg_keys[5], 1), 0, NPASS - 1).astype(jnp.int32),
        "negative_ids": set_ends(jax.random.randint(arg_keys[6], (QUERIES, NEG), 0, NPASS), jax.random.fold_in(arg_keys[6], 1), 0, NPASS - 1).astype(jnp.int32),
        "margins": bell_draw(arg_keys[7], (QUERIES, NEG), 1.0, 6.0, ((0, 8),), jnp.float32),
        "pair_counts": draw_pair_counts(jax.random.fold_in(arg_keys[9], 71), 0),
    }


def block_hidden(inputs, o_weight):
    ctx_block, res_block = inputs
    width = D // N_TENSOR
    ctx_groups = ctx_block.reshape(ctx_block.shape[0], N_TENSOR, width).transpose(1, 0, 2)
    weight_groups = o_weight.reshape(N_TENSOR, width, D)

    def add_group(total, pair):
        part = jnp.dot(pair[0], pair[1], preferred_element_type=jnp.float32)
        return (total + part, None)
    start = jnp.zeros((ctx_block.shape[0], D), jnp.float32)
    total, _ = lax.scan(add_group, start, (ctx_groups, weight_groups))
    return res_block.astype(jnp.float32) + total

def reference(context, resid, o_weight, norm_gain, queries, positive_ids, negative_ids, margins, pair_counts):
    rows = PASS_DEV * SEQ
    ctx_blocks = context.reshape(N_DP, rows, D)
    res_blocks = resid.reshape(N_DP, rows, D)
    hidden = lax.map(lambda pair: block_hidden(pair, o_weight), (ctx_blocks, res_blocks))
    inv = lax.rsqrt(lax.optimization_barrier(jnp.mean(hidden * hidden, axis=-1, keepdims=True)) + 1e-05)
    normed = hidden * inv * norm_gain
    pooled = lax.optimization_barrier(jnp.sum(normed.reshape(N_DP * PASS_DEV, SEQ, D), axis=1))
    scale = 1.0 / jnp.sqrt(jnp.float32(D * SEQ))
    scores = jnp.dot(queries, pooled.T, precision=lax.Precision.HIGHEST) * scale
    npass = N_DP * PASS_DEV
    nquery = N_DP * Q_DEV
    passes = jnp.arange(npass, dtype=jnp.int32)
    onehot_pos = (positive_ids[:, None] == passes[None, :]).astype(jnp.float32)
    onehot_neg = (negative_ids[:, :, None] == passes[None, None, :]).astype(jnp.float32)
    score_pos = lax.optimization_barrier(jnp.sum(onehot_pos * scores, axis=-1))
    score_neg = lax.optimization_barrier(jnp.sum(onehot_neg * scores[:, None, :], axis=-1))
    err = score_pos[:, None] - score_neg - margins
    live = (jnp.arange(NEG, dtype=jnp.int32)[None, :] < pair_counts[:, None]).astype(jnp.float32)
    counts = pair_counts.astype(jnp.float32)
    loss = jnp.sum(lax.optimization_barrier(jnp.sum(live * err * err, axis=1)) / counts) / nquery
    weight = 2.0 * live * err / (counts[:, None] * nquery)
    coef = onehot_pos * lax.optimization_barrier(jnp.sum(weight, axis=1))[:, None] - lax.optimization_barrier(jnp.sum(weight[:, :, None] * onehot_neg, axis=1))
    pass_grad = jnp.dot(coef.T, queries, precision=lax.Precision.HIGHEST) * scale
    token_grad = jnp.repeat(pass_grad, SEQ, axis=0).reshape(N_DP, rows, D)
    upward = token_grad * norm_gain
    inner = lax.optimization_barrier(jnp.mean(hidden * upward, axis=-1, keepdims=True))
    grad = 65536.0 * (inv * upward - hidden * inv * inv * inv * inner)
    return (grad.reshape(npass * SEQ, D), loss)
```

```python
import jax
import jax.numpy as jnp
from jax import lax
from jax.sharding import PartitionSpec as P

D = 7168
SEQ = 512
PASS_DEV = 2
Q_DEV = 4
NEG = 7


def shards(
    context, resid, o_weight, norm_gain, queries, positive_ids, negative_ids, margins, pair_counts
):
    full_weight = lax.all_gather(o_weight, "dp", axis=1, tiled=True)
    tok_rows = resid.shape[0]
    attn = lax.psum_scatter(
        jnp.dot(context, full_weight, preferred_element_type=jnp.float32),
        "tensor",
        scatter_dimension=0,
        tiled=True,
    )
    hidden = resid.astype(jnp.float32) + attn
    inv = lax.rsqrt(jnp.mean(hidden * hidden, axis=-1, keepdims=True) + 1e-05)
    normed = hidden * inv * norm_gain
    first = lax.axis_index("tensor") * tok_rows
    passage_of = (first + jnp.arange(tok_rows, dtype=jnp.int32)) // SEQ
    member = (passage_of[None, :] == jnp.arange(PASS_DEV, dtype=jnp.int32)[:, None]).astype(
        jnp.float32
    )
    partial_value = jnp.dot(member, normed, precision=lax.Precision.HIGHEST)
    scale = 1.0 / jnp.sqrt(jnp.float32(D * SEQ))
    npass = PASS_DEV * lax.axis_size("dp")
    nquery = Q_DEV * lax.axis_size("dp")
    pooled = lax.psum(partial_value, "tensor")
    every_pass = lax.all_gather(pooled, "dp", axis=0, tiled=True)
    scores = jnp.dot(queries, every_pass.T, precision=lax.Precision.HIGHEST) * scale
    passes = jnp.arange(npass, dtype=jnp.int32)
    onehot_pos = (positive_ids[:, None] == passes[None, :]).astype(jnp.float32)
    onehot_neg = (negative_ids[:, :, None] == passes[None, None, :]).astype(jnp.float32)
    score_pos = jnp.sum(onehot_pos * scores, axis=-1)
    score_neg = jnp.sum(onehot_neg * scores[:, None, :], axis=-1)
    err = score_pos[:, None] - score_neg - margins
    live = (jnp.arange(NEG, dtype=jnp.int32)[None, :] < pair_counts[:, None]).astype(jnp.float32)
    counts = pair_counts.astype(jnp.float32)
    local_loss = jnp.sum(jnp.sum(live * err * err, axis=1) / counts) / nquery
    weight = 2.0 * live * err / (counts[:, None] * nquery)
    coef = onehot_pos * jnp.sum(weight, axis=1)[:, None] - jnp.sum(
        weight[:, :, None] * onehot_neg, axis=1
    )
    grad_terms = jnp.dot(coef.T, queries, precision=lax.Precision.HIGHEST) * scale
    pass_grad = lax.psum_scatter(grad_terms, "dp", scatter_dimension=0, tiled=True)
    loss = lax.psum(local_loss, "dp")
    upward = jnp.dot(member.T, pass_grad, precision=lax.Precision.HIGHEST) * norm_gain
    inner = jnp.mean(hidden * upward, axis=-1, keepdims=True)
    grad = 65536.0 * (inv * upward - hidden * inv * inv * inv * inner)
    return (grad, loss)


def line_shards(
    context, resid, o_weight, norm_gain, queries, positive_ids, negative_ids, margins, pair_counts
):
    f32 = jnp.float32
    dp_at, t_at = lax.axis_index("dp"), lax.axis_index("tensor")
    z, x = dp_at // 2, dp_at % 2
    y, core = t_at // 2, t_at % 2
    tok_rows = resid.shape[0]
    width = o_weight.shape[1]

    def shift(value, step, sources):
        pairs = [(2 * s + i, 2 * (s + step) + i) for s in sources for i in range(2)]
        return lax.ppermute(value, "dp", pairs)

    def swap_x(value, zs):
        pairs = [(2 * s + i, 2 * s + 1 - i) for s in zs for i in range(2)]
        return lax.ppermute(value, "dp", pairs)

    def swap_tensor(value, bit, zs):
        pairs = [
            ((2 * s + i) * 4 + t, (2 * s + i) * 4 + (t ^ bit))
            for s in zs
            for i in range(2)
            for t in range(4)
        ]
        return lax.ppermute(value, ("dp", "tensor"), pairs)

    rows = context.reshape(2, 2, tok_rows, context.shape[1])
    rows = jnp.where(y == 0, rows, rows[::-1])
    rows = jnp.where(core == 0, rows, rows[:, ::-1])
    mine = rows.transpose(1, 0, 2, 3).reshape(context.shape)
    every = (0, 1, 2, 3)
    theirs = swap_x(mine, every)

    small = jnp.concatenate(
        [
            queries,
            positive_ids.astype(f32)[:, None],
            negative_ids.astype(f32),
            margins,
            pair_counts.astype(f32)[:, None],
        ],
        axis=1,
    )
    small = lax.all_gather(small, "dp", axis=0, tiled=True)
    queries = small[:, :D]
    positive_ids = small[:, D].astype(jnp.int32)
    negative_ids = small[:, D + 1 : D + 1 + NEG].astype(jnp.int32)
    margins = small[:, D + 1 + NEG : D + 1 + 2 * NEG]
    counts = small[:, D + 1 + 2 * NEG]

    left1 = shift(o_weight, 1, (0, 1, 2))
    right1 = shift(o_weight, -1, (1, 2, 3))
    left2 = shift(left1, 1, (1, 2))
    right2 = shift(right1, -1, (1, 2))
    left3 = shift(left2, 1, (2,))
    right3 = shift(right2, -1, (1,))

    def reduced(acts, block, zs):
        part = jnp.dot(acts, block, preferred_element_type=f32)
        half, quarter = 2 * tok_rows, tok_rows
        kept = part[:half] + swap_tensor(part[half:], 1, every)
        return kept[:quarter] + swap_tensor(kept[quarter:], 2, zs)

    def columns(block, zs):
        away = swap_x(reduced(theirs, block, zs), zs)
        return reduced(mine, block, zs), away

    own = columns(o_weight, every)
    from_left = columns(left1, (1, 2, 3))
    from_right = columns(right1, (0, 1, 2))
    opposite = columns(jnp.where(z >= 2, left2, right2), every)
    far = columns(jnp.where(z == 3, left3, right3), (0, 3))
    before = [jnp.where(z == 0, a, b) for a, b in zip(far, from_left)]
    after = [jnp.where(z == 3, a, b) for a, b in zip(far, from_right)]
    blocks = jnp.stack([*own, *after, *opposite, *before])
    ordered = [
        lax.dynamic_index_in_dim(blocks, ((j // 2 - z) % 4) * 2 + (j + x) % 2, 0, keepdims=False)
        for j in range(8)
    ]
    hidden = resid.astype(f32) + jnp.concatenate(ordered, axis=1)
    inv = lax.rsqrt(jnp.mean(hidden * hidden, axis=-1, keepdims=True) + 1e-05)
    pooled = jnp.sum(hidden * inv, axis=0) * norm_gain
    scale = 1.0 / jnp.sqrt(f32(D * SEQ))
    npass = PASS_DEV * lax.axis_size("dp")
    nquery = Q_DEV * lax.axis_size("dp")
    passes = jnp.arange(npass, dtype=jnp.int32)
    passage = PASS_DEV * dp_at + (t_at * tok_rows) // SEQ
    here = (passes == passage).astype(f32)
    scores = jnp.sum(queries * pooled[None, :], axis=1)[:, None] * here[None, :] * scale
    scores = lax.psum(scores, ("dp", "tensor"))
    onehot_pos = (positive_ids[:, None] == passes[None, :]).astype(f32)
    onehot_neg = (negative_ids[:, :, None] == passes[None, None, :]).astype(f32)
    score_pos = jnp.sum(onehot_pos * scores, axis=-1)
    score_neg = jnp.sum(onehot_neg * scores[:, None, :], axis=-1)
    err = score_pos[:, None] - score_neg - margins
    live = (jnp.arange(NEG, dtype=f32)[None, :] < counts[:, None]).astype(f32)
    loss = jnp.sum(jnp.sum(live * err * err, axis=1) / counts) / nquery
    weight = 2.0 * live * err / (counts[:, None] * nquery)
    at_pos = jnp.sum(onehot_pos * here[None, :], axis=1)
    at_neg = jnp.sum(onehot_neg * here[None, None, :], axis=2)
    coef = at_pos * jnp.sum(weight, axis=1) - jnp.sum(weight * at_neg, axis=1)
    pass_grad = jnp.sum(coef[:, None] * queries, axis=0) * scale
    upward = (pass_grad * norm_gain)[None, :]
    inner = jnp.mean(hidden * upward, axis=-1, keepdims=True)
    grad = 65536.0 * (inv * upward - hidden * (inv * inv * inv * inner))
    return (grad, loss)


def solution(mesh):
    body = line_shards if dict(mesh.shape) == {"dp": 8, "tensor": 4} else shards
    return jax.shard_map(
        body,
        mesh=mesh,
        in_specs=(
            P("dp", "tensor"),
            P(("dp", "tensor"), None),
            P("tensor", "dp"),
            P(),
            P("dp", None),
            P("dp"),
            P("dp", None),
            P("dp", None),
            P("dp"),
        ),
        out_specs=(P(("dp", "tensor"), None), P()),
        check_vma=False,
    )
```
